32 devices in a mesh: branch: 2 (over x), sample: 16 (over z, y, core).
Axes of the slice: x: 2, y: 2, z: 4, core: 2. Of those that a mesh axis runs over, the one named last changes fastest.
Arguments:
- abundance: bfloat16 [128, 32768], P('sample', 'branch'), may hold values from 0.01 to 100, as said below
- length_table: float32 [32768], P('branch'), may hold values from 0.01 to 1, as said below
- branch_rows: int32 [32768], P('branch'), may hold values from 0 to 16383, as said below
Outputs:
- distance: float32 [128, 128], P('sample', 'branch')
The draws below stay inside these ranges and needn't reach their ends.
Inputs may be any that keep to these rules, and one draw needn't show every extreme that they name: `abundance`: entries are positive. `length_table`: positive branch lengths. `branch_rows`: within each aligned block of 16384 entries every number from 0 to 16383 appears once.
All inputs are finite; a program needn't handle non-finite values.
Results may differ from the reference program's by a relative error of at most 0.0003.
Values may be sent and summed in bfloat16 or wider, within the bound.
A program may use at most 64 MiB of HBM per device.

```python
import jax
import jax.numpy as jnp
from jax import lax

BRANCHES = 32768
SAMPLES = 128
N_BRANCH = 2


def group_width():
    return max(min(256, BRANCHES // 64), 1)


def group_lengths(key):
    group_count = BRANCHES // group_width()
    length_key = jax.random.fold_in(key, 31)
    return jnp.exp(jax.random.uniform(length_key, (group_count,), jnp.float32, jnp.log(0.02), jnp.log(0.5)))


def row_orders(key):
    per_group = BRANCHES // N_BRANCH
    keys = jax.random.split(jax.random.fold_in(key, 21), N_BRANCH)
    orders = jax.vmap(lambda single: jax.random.permutation(single, per_group))(keys)
    return orders.reshape(-1).astype(jnp.int32)


def draw_abundance(key, part):
    width = group_width()
    group_count = BRANCHES // width
    spans = group_lengths(key)
    level = (jnp.log(spans) - jnp.log(0.02)) / jnp.log(25.0)
    spread = jnp.log(100.0) * (1.0 - level) + jnp.log(2.0) * level
    scale_key = jax.random.fold_in(key, 11)
    value_key = jax.random.fold_in(key, 12)
    unit = jax.random.uniform(scale_key, (SAMPLES, group_count), jnp.float32, 0.0, 1.0)
    scales = jnp.exp(unit * spread[None, :])
    scales = jnp.repeat(scales, width, axis=1)
    base = jnp.exp(jax.random.uniform(value_key, (SAMPLES, BRANCHES), jnp.float32, jnp.log(0.01), 0.0))
    rising = 3.0 ** (jnp.arange(BRANCHES, dtype=jnp.float32) / BRANCHES)
    result = jnp.clip(base * scales * rising[None, :], 0.01, 100.0)
    return result.astype(jnp.bfloat16)


def draw_length_table(key, part):
    width = group_width()
    spans = jnp.repeat(group_lengths(key), width)
    rough_key = jax.random.fold_in(key, 41)
    rough = jnp.exp(jax.random.uniform(rough_key, (BRANCHES,), jnp.float32, jnp.log(0.5), jnp.log(2.0)))
    per_branch = jnp.clip(spans * rough, 0.01, 1.0)
    per_group = BRANCHES // N_BRANCH
    offsets = jnp.arange(BRANCHES, dtype=jnp.int32) // per_group * per_group
    places = (offsets + row_orders(key)).astype(jnp.int32)
    table = jnp.zeros((BRANCHES,), jnp.float32).at[places].set(per_branch)
    return table.astype(jnp.float32)


def draw_branch_rows(key, part):
    return row_orders(key)


def setup_inputs(seed: int = 0) -> dict:
    key_of = jax.random.split(jax.random.key(seed), 4)
    return {
        "abundance": draw_abundance(jax.random.fold_in(key_of[3], 71), 0),
        "length_table": draw_length_table(jax.random.fold_in(key_of[3], 71), 0),
        "branch_rows": draw_branch_rows(jax.random.fold_in(key_of[3], 71), 0),
    }


def reference(abundance, length_table, branch_rows):
    values = abundance.astype(jnp.float32)
    totals = lax.optimization_barrier(jnp.sum(values, axis=1))
    shares = (values / totals[:, None]).astype(jnp.bfloat16)
    per_group = BRANCHES // N_BRANCH
    offsets = jnp.arange(BRANCHES, dtype=jnp.int32) // per_group * per_group
    lengths = length_table[(offsets + branch_rows).astype(jnp.int32)]
    columns = shares.T
    block_size = 128
    block_count = BRANCHES // block_size

    def row_block(index):
        mine = lax.dynamic_slice_in_dim(columns, (index * 16).astype(jnp.int32), 16, 1)

        def absorb(carry, turn):
            begin = (turn * block_size).astype(jnp.int32)
            left = lax.dynamic_slice_in_dim(mine, begin, block_size, 0).astype(jnp.float32)[:, :, None]
            right = lax.dynamic_slice_in_dim(columns, begin, block_size, 0).astype(jnp.float32)[:, None, :]
            weight = lax.dynamic_slice_in_dim(lengths, begin, block_size, 0)[:, None, None]
            summed = left + right
            inverse = lax.rsqrt(summed)
            return ((carry[0] + lax.optimization_barrier(jnp.sum(weight * jnp.abs(left - right) * inverse, axis=0)), carry[1] + lax.optimization_barrier(jnp.sum(weight * summed * inverse, axis=0))), None)
        empty = jnp.zeros((16, SAMPLES), jnp.float32)
        result, unused = lax.scan(absorb, (empty, empty), jnp.arange(block_count, dtype=jnp.int32))
        return result
    numer, denom = lax.map(row_block, jnp.arange(SAMPLES // 16, dtype=jnp.int32))
    numer = numer.reshape(SAMPLES, SAMPLES)
    denom = denom.reshape(SAMPLES, SAMPLES)
    return numer / denom
```

```python
import functools

import jax
import jax.numpy as jnp
from jax import lax
from jax.experimental import pallas as pl
from jax.experimental.pallas import tpu as pltpu
from jax.sharding import PartitionSpec as P

MESH = pl.DeviceIdType.MESH
F32 = jnp.float32
ROWS = 8
LANES = 128


def pair_sums(mine, other, lengths):
    count, width = mine.shape
    others = other.shape[0]
    block_size = width
    while block_size > 512 and block_size % 2 == 0 and (block_size * count * others > 2097152):
        block_size = block_size // 2
    block_count = width // block_size

    def absorb(carry, turn):
        begin = turn * block_size
        left = lax.dynamic_slice_in_dim(mine, begin, block_size, 1).astype(F32)[:, None, :]
        right = lax.dynamic_slice_in_dim(other, begin, block_size, 1).astype(F32)[None, :, :]
        weight = lax.dynamic_slice_in_dim(lengths, begin, block_size, 0)[None, None, :]
        summed = left + right
        inverse = lax.rsqrt(summed)
        return (
            (
                carry[0] + jnp.sum(weight * jnp.abs(left - right) * inverse, axis=2),
                carry[1] + jnp.sum(weight * summed * inverse, axis=2),
            ),
            None,
        )

    empty = jnp.zeros((count, others), F32)
    result, unused = lax.scan(absorb, (empty, empty), jnp.arange(block_count, dtype=jnp.int32))
    return result


def plain_body(abundance, length_table, branch_rows):
    values = abundance.astype(F32)
    totals = lax.psum(jnp.sum(values, axis=1), "branch")
    shares = (values / totals[:, None]).astype(jnp.bfloat16)
    lengths = jnp.take(length_table, branch_rows)
    numer_part, denom_part = pair_sums(
        shares, lax.all_gather(shares, "sample", axis=0, tiled=True), lengths
    )
    summed = (
        lax.psum_scatter(numer_part, "branch", scatter_dimension=1, tiled=True),
        lax.psum_scatter(denom_part, "branch", scatter_dimension=1, tiled=True),
    )
    return summed[0] / summed[1]


def kernel(
    axes, n_branch, n_sample, chunk,
    ab_hbm, table_hbm, rows_hbm, out_ref,
    ab, table, rows, x_buf, tot_send, tot_buf, p_ref, l2_ref, big, den, res_send, res_buf,
    local_sem, own_sem, x_send_sem, x_recv_sem, t_send_sem, t_recv_sem, r_send_sem, r_recv_sem,
):
    n_dev = n_branch * n_sample
    depth = chunk // LANES
    half = n_sample * ROWS // n_branch
    my_t = lax.axis_index("branch")
    my_s = lax.axis_index("sample")
    me = my_t * n_sample + my_s

    def place(t, s):
        where = {"branch": t, "sample": s}
        return tuple(where[name] for name in axes)

    def peer_at(k):
        flat = lax.rem(me + k, n_dev)
        return flat, flat // n_sample, lax.rem(flat, n_sample)

    ab_copy = pltpu.make_async_copy(ab_hbm, ab, local_sem.at[0])
    table_copy = pltpu.make_async_copy(table_hbm, table, local_sem.at[1])
    rows_copy = pltpu.make_async_copy(rows_hbm.at[my_s], rows, local_sem.at[2])
    own_copy = pltpu.make_async_copy(
        ab_hbm.at[:, pl.ds(pl.multiple_of(my_s * chunk, chunk), chunk)], x_buf.at[my_s], own_sem
    )
    ab_copy.start()
    table_copy.start()
    rows_copy.start()
    own_copy.start()

    barrier = pltpu.get_barrier_semaphore()

    def greet(k, carry):
        flat, t, s = peer_at(k)
        pl.semaphore_signal(barrier, inc=1, device_id=place(t, s), device_id_type=MESH)
        return carry

    lax.fori_loop(1, n_dev, greet, 0)
    pl.semaphore_wait(barrier, n_dev - 1)

    def x_copy(to_s, slot, recv):
        return pltpu.make_async_remote_copy(
            src_ref=ab_hbm.at[:, pl.ds(pl.multiple_of(to_s * chunk, chunk), chunk)],
            dst_ref=x_buf.at[slot],
            send_sem=x_send_sem.at[to_s],
            recv_sem=x_recv_sem.at[recv],
            device_id=place(my_t, to_s),
            device_id_type=MESH,
        )

    def send_x(k, carry):
        x_copy(lax.rem(my_s + k, n_sample), my_s, my_s).start()
        return carry

    lax.fori_loop(1, n_sample, send_x, 0)

    lane = lax.broadcasted_iota(jnp.int32, (ROWS, LANES), 1)
    sub = lax.broadcasted_iota(jnp.int32, (ROWS, LANES), 0)
    eye = lane == sub

    ab_copy.wait()
    step = min(chunk, 1024)

    def add_up(turn, acc):
        return acc + ab[:, pl.ds(pl.multiple_of(turn * step, step), step)].astype(F32)

    acc = lax.fori_loop(0, n_sample * chunk // step, add_up, jnp.zeros((ROWS, step), F32))
    part = jnp.sum(acc, axis=1, keepdims=True)
    line = jnp.sum(jnp.where(eye, part, 0.0), axis=0, keepdims=True)
    tot_send[...] = line
    tot_buf[me] = line

    def t_copy(flat, t, s, slot):
        return pltpu.make_async_remote_copy(
            src_ref=tot_send,
            dst_ref=tot_buf.at[slot],
            send_sem=t_send_sem.at[flat],
            recv_sem=t_recv_sem.at[slot],
            device_id=place(t, s),
            device_id_type=MESH,
        )

    def send_t(k, carry):
        flat, t, s = peer_at(k)
        t_copy(flat, t, s, me).start()
        return carry

    lax.fori_loop(1, n_dev, send_t, 0)

    table_copy.wait()
    rows_copy.wait()
    index = rows[...]
    high, low = index // LANES, index % LANES

    def look_up(h, found):
        line = jnp.broadcast_to(table[pl.ds(h, 1), :], (depth, LANES))
        picked = jnp.take_along_axis(line, low, axis=1, mode="promise_in_bounds")
        return jnp.where(high == h, picked, found)

    lengths = lax.fori_loop(
        0, table.shape[0], look_up, jnp.zeros((depth, LANES), F32), unroll=8
    )
    l2_ref[...] = lengths * lengths

    def await_t(k, carry):
        flat, t, s = peer_at(k)
        t_copy(flat, t, s, flat).wait()
        return carry

    lax.fori_loop(1, n_dev, await_t, 0)
    own_copy.wait()

    def await_x(k, carry):
        s = lax.rem(my_s + k, n_sample)
        x_copy(s, s, s).wait()
        return carry

    lax.fori_loop(1, n_sample, await_x, 0)

    def prepare(s, carry):
        total = tot_buf[s]
        for t in range(1, n_branch):
            total = total + tot_buf[t * n_sample + s]
        column = jnp.sum(
            jnp.where(eye, jnp.broadcast_to(total, (ROWS, LANES)), 0.0), axis=1, keepdims=True
        )
        for r in range(depth):
            values = x_buf[s, :, r * LANES:(r + 1) * LANES].astype(F32)
            shares = (values / column).astype(jnp.bfloat16).astype(F32)
            p_ref[s, r] = shares * l2_ref[r:r + 1, :]
        return carry

    lax.fori_loop(0, n_sample, prepare, 0)

    big[...] = jnp.zeros_like(big)
    den[...] = jnp.zeros_like(den)
    pair_count = n_sample * (n_sample + 1) // 2

    def split(turn):
        j = lax.rem(turn, n_sample)
        return lax.rem(j + turn // n_sample, n_sample), j

    def place_sums(turn, sums):
        i_block, j_block = split(turn)
        now_big, now_den = big[j_block], den[j_block]
        for i in range(ROWS):
            here = lane == i_block * ROWS + i
            now_big = jnp.where(here, jnp.sum(sums[i], axis=1, keepdims=True), now_big)
            now_den = jnp.where(here, jnp.sum(sums[ROWS + i], axis=1, keepdims=True), now_den)
        big[j_block] = now_big
        den[j_block] = now_den

    def pairs(turn):
        i_block, j_block = split(turn)
        sums = [None] * (2 * ROWS)
        for r in range(depth):
            q = p_ref[j_block, r]
            for i in range(ROWS):
                p = p_ref[i_block, r, pl.ds(i, 1), :]
                summed = p + q
                inverse = lax.rsqrt(summed)
                top = jnp.maximum(p, q) * inverse
                low_part = summed * inverse
                if r == 0:
                    sums[i], sums[ROWS + i] = top, low_part
                else:
                    sums[i] += top
                    sums[ROWS + i] += low_part
        return tuple(sums)

    def advance(turn, sums):
        place_sums(turn - 1, sums)
        return pairs(turn)

    place_sums(pair_count - 1, lax.fori_loop(1, pair_count, advance, pairs(0)))

    full = (n_sample * ROWS, LANES)
    row_block = lax.broadcasted_iota(jnp.int32, full, 0) // ROWS
    column_block = lax.broadcasted_iota(jnp.int32, full, 1) // ROWS
    apart = (column_block - row_block + n_sample) % n_sample
    mine = (2 * apart < n_sample) | ((2 * apart == n_sample) & (2 * row_block < n_sample))
    whole_big = big[...].reshape(full)
    whole_den = den[...].reshape(full)
    whole_big = jnp.where(mine, whole_big, whole_big.T)
    whole_den = jnp.where(mine, whole_den, whole_den.T)
    first = lax.broadcasted_iota(jnp.int32, full, 1) < half
    for t in range(n_branch):
        left = pltpu.roll(whole_big, (LANES - t * half) % LANES, 1) if t else whole_big
        shift = (LANES + half - t * half) % LANES
        right = pltpu.roll(whole_den, shift, 1) if shift else whole_den
        res_send[t] = jnp.where(first, left, right).reshape(n_sample, ROWS, LANES)

    def r_copy(flat, t, s, slot):
        return pltpu.make_async_remote_copy(
            src_ref=res_send.at[t, s],
            dst_ref=res_buf.at[slot],
            send_sem=r_send_sem.at[flat],
            recv_sem=r_recv_sem.at[slot],
            device_id=place(t, s),
            device_id_type=MESH,
        )

    def send_r(k, carry):
        flat, t, s = peer_at(k)
        r_copy(flat, t, s, me).start()
        return carry

    lax.fori_loop(1, n_dev, send_r, 0)
    res_buf[me] = res_send[my_t, my_s]

    def await_r(k, carry):
        flat, t, s = peer_at(k)
        r_copy(flat, t, s, flat).wait()
        return carry

    lax.fori_loop(1, n_dev, await_r, 0)
    total = res_buf[0]
    for k in range(1, n_dev):
        total = total + res_buf[k]
    out_ref[...] = total


def kernel_body(axes, n_branch, n_sample, abundance, length_table, branch_rows):
    width = abundance.shape[1]
    chunk = width // n_sample
    depth = chunk // LANES
    n_dev = n_branch * n_sample
    half = n_sample * ROWS // n_branch
    sums = pl.pallas_call(
        functools.partial(kernel, axes, n_branch, n_sample, chunk),
        out_shape=jax.ShapeDtypeStruct((ROWS, LANES), F32),
        in_specs=[pl.BlockSpec(memory_space=pl.ANY)] * 3,
        out_specs=pl.BlockSpec(memory_space=pltpu.VMEM),
        scratch_shapes=[
            pltpu.VMEM((ROWS, width), jnp.bfloat16),
            pltpu.VMEM((width // LANES, LANES), F32),
            pltpu.VMEM((depth, LANES), jnp.int32),
            pltpu.VMEM((n_sample, ROWS, chunk), jnp.bfloat16),
            pltpu.VMEM((1, LANES), F32),
            pltpu.VMEM((n_dev, 1, LANES), F32),
            pltpu.VMEM((n_sample, depth, ROWS, LANES), F32),
            pltpu.VMEM((depth, LANES), F32),
            pltpu.VMEM((n_sample, ROWS, LANES), F32),
            pltpu.VMEM((n_sample, ROWS, LANES), F32),
            pltpu.VMEM((n_branch, n_sample, ROWS, LANES), F32),
            pltpu.VMEM((n_dev, ROWS, LANES), F32),
            pltpu.SemaphoreType.DMA((3,)),
            pltpu.SemaphoreType.DMA,
            pltpu.SemaphoreType.DMA((n_sample,)),
            pltpu.SemaphoreType.DMA((n_sample,)),
            pltpu.SemaphoreType.DMA((n_dev,)),
            pltpu.SemaphoreType.DMA((n_dev,)),
            pltpu.SemaphoreType.DMA((n_dev,)),
            pltpu.SemaphoreType.DMA((n_dev,)),
        ],
        compiler_params=pltpu.CompilerParams(collective_id=0, has_side_effects=True),
    )(
        abundance,
        length_table.reshape(width // LANES, LANES),
        branch_rows.reshape(n_sample, depth, LANES),
    )
    big, den = sums[:, :half], sums[:, half:2 * half]
    return (2.0 * big - den) / den


def solution(mesh):
    n_branch, n_sample = mesh.shape["branch"], mesh.shape["sample"]
    axes = tuple(mesh.axis_names)

    def body(abundance, length_table, branch_rows):
        rows, width = abundance.shape
        fits = (
            rows == ROWS
            and n_sample * ROWS == LANES
            and n_branch > 1
            and LANES % n_branch == 0
            and width % (n_sample * ROWS * LANES) == 0
        )
        if not fits:
            return plain_body(abundance, length_table, branch_rows)
        return kernel_body(axes, n_branch, n_sample, abundance, length_table, branch_rows)

    placed = (P("sample", "branch"), P("branch"), P("branch"))
    return jax.shard_map(
        body, mesh=mesh, in_specs=placed, out_specs=P("sample", "branch"), check_vma=False
    )
```

```python
import functools

import jax
import jax.numpy as jnp
from jax import lax
from jax.experimental import pallas as pl
from jax.experimental.pallas import tpu as pltpu
from jax.sharding import PartitionSpec as P

MESH = pl.DeviceIdType.MESH
F32 = jnp.float32
ROWS = 8
LANES = 128
UNROLL = 5


def pair_sums(mine, other, lengths):
    count, width = mine.shape
    others = other.shape[0]
    block_size = width
    while block_size > 512 and block_size % 2 == 0 and (block_size * count * others > 2097152):
        block_size = block_size // 2
    block_count = width // block_size

    def absorb(carry, turn):
        begin = turn * block_size
        left = lax.dynamic_slice_in_dim(mine, begin, block_size, 1).astype(F32)[:, None, :]
        right = lax.dynamic_slice_in_dim(other, begin, block_size, 1).astype(F32)[None, :, :]
        weight = lax.dynamic_slice_in_dim(lengths, begin, block_size, 0)[None, None, :]
        summed = left + right
        inverse = lax.rsqrt(summed)
        return (
            (
                carry[0] + jnp.sum(weight * jnp.abs(left - right) * inverse, axis=2),
                carry[1] + jnp.sum(weight * summed * inverse, axis=2),
            ),
            None,
        )

    empty = jnp.zeros((count, others), F32)
    result, unused = lax.scan(absorb, (empty, empty), jnp.arange(block_count, dtype=jnp.int32))
    return result


def plain_body(abundance, length_table, branch_rows):
    values = abundance.astype(F32)
    totals = lax.psum(jnp.sum(values, axis=1), "branch")
    shares = (values / totals[:, None]).astype(jnp.bfloat16)
    lengths = jnp.take(length_table, branch_rows)
    numer_part, denom_part = pair_sums(
        shares, lax.all_gather(shares, "sample", axis=0, tiled=True), lengths
    )
    summed = (
        lax.psum_scatter(numer_part, "branch", scatter_dimension=1, tiled=True),
        lax.psum_scatter(denom_part, "branch", scatter_dimension=1, tiled=True),
    )
    return summed[0] / summed[1]


def kernel(
    axes, n_branch, n_sample, chunk,
    ab_hbm, table_hbm, rows_hbm, out_ref,
    ab, table, rows, x_buf, tot_send, tot_buf, p_ref, l2_ref, big, den, res_send, res_buf,
    local_sem, own_sem, x_send_sem, x_recv_sem, t_send_sem, t_recv_sem, r_send_sem, r_recv_sem,
):
    n_dev = n_branch * n_sample
    depth = chunk // LANES
    half = n_sample * ROWS // n_branch
    my_t = lax.axis_index("branch")
    my_s = lax.axis_index("sample")
    me = my_t * n_sample + my_s

    def place(t, s):
        where = {"branch": t, "sample": s}
        return tuple(where[name] for name in axes)

    def peer_at(k):
        flat = lax.bitwise_xor(me, k)
        return flat, flat // n_sample, lax.rem(flat, n_sample)

    ab_copy = pltpu.make_async_copy(ab_hbm, ab, local_sem.at[0])
    table_copy = pltpu.make_async_copy(table_hbm, table, local_sem.at[1])
    rows_copy = pltpu.make_async_copy(rows_hbm.at[my_s], rows, local_sem.at[2])
    own_copy = pltpu.make_async_copy(
        ab_hbm.at[:, pl.ds(pl.multiple_of(my_s * chunk, chunk), chunk)], x_buf.at[my_s], own_sem
    )
    ab_copy.start()
    table_copy.start()
    rows_copy.start()
    own_copy.start()

    barrier = pltpu.get_barrier_semaphore()

    def greet(k, carry):
        flat, t, s = peer_at(k)
        pl.semaphore_signal(barrier, inc=1, device_id=place(t, s), device_id_type=MESH)
        return carry

    lax.fori_loop(1, n_dev, greet, 0)

    def x_copy(to_s, slot, recv):
        return pltpu.make_async_remote_copy(
            src_ref=ab_hbm.at[:, pl.ds(pl.multiple_of(to_s * chunk, chunk), chunk)],
            dst_ref=x_buf.at[slot],
            send_sem=x_send_sem.at[to_s],
            recv_sem=x_recv_sem.at[recv],
            device_id=place(my_t, to_s),
            device_id_type=MESH,
        )

    def send_x(k, carry):
        x_copy(lax.bitwise_xor(my_s, k), my_s, my_s).start()
        return carry

    lane = lax.broadcasted_iota(jnp.int32, (ROWS, LANES), 1)
    sub = lax.broadcasted_iota(jnp.int32, (ROWS, LANES), 0)
    eye = lane == sub

    ab_copy.wait()
    step = min(chunk, 1024)

    def add_up(turn, acc):
        return acc + ab[:, pl.ds(pl.multiple_of(turn * step, step), step)].astype(F32)

    acc = lax.fori_loop(0, n_sample * chunk // step, add_up, jnp.zeros((ROWS, step), F32))
    part = jnp.sum(acc, axis=1, keepdims=True)
    line = jnp.sum(jnp.where(eye, part, 0.0), axis=0, keepdims=True)
    tot_send[...] = line
    tot_buf[me] = line

    def t_copy(flat, t, s, slot):
        return pltpu.make_async_remote_copy(
            src_ref=tot_send,
            dst_ref=tot_buf.at[slot],
            send_sem=t_send_sem.at[flat],
            recv_sem=t_recv_sem.at[slot],
            device_id=place(t, s),
            device_id_type=MESH,
        )

    def send_t(k, carry):
        flat, t, s = peer_at(k)
        t_copy(flat, t, s, me).start()
        return carry


    table_copy.wait()
    rows_copy.wait()
    index = rows[...]
    high, low = index // LANES, index % LANES

    def look_up(h, found):
        line = jnp.broadcast_to(table[pl.ds(h, 1), :], (depth, LANES))
        picked = jnp.take_along_axis(line, low, axis=1, mode="promise_in_bounds")
        return jnp.where(high == h, picked, found)

    lengths = lax.fori_loop(
        0, table.shape[0], look_up, jnp.zeros((depth, LANES), F32), unroll=8
    )
    l2_ref[...] = lengths * lengths

    pl.semaphore_wait(barrier, n_dev - 1)
    lax.fori_loop(1, n_dev, send_t, 0)
    lax.fori_loop(1, n_sample, send_x, 0)

    near = n_sample // 2

    def arrive(k, carry):
        s = lax.bitwise_xor(my_s, k)
        for t in range(n_branch):
            flat = t * n_sample + s

            @pl.when(flat != me)
            def _():
                t_copy(flat, t, s, flat).wait()

        @pl.when(k > 0)
        def _():
            x_copy(s, s, s).wait()

        return carry

    def prepare(k, carry):
        s = lax.bitwise_xor(my_s, k)
        total = tot_buf[s]
        for t in range(1, n_branch):
            total = total + tot_buf[t * n_sample + s]
        column = jnp.sum(
            jnp.where(eye, jnp.broadcast_to(total, (ROWS, LANES)), 0.0), axis=1, keepdims=True
        )
        for r in range(depth):
            values = x_buf[s, :, r * LANES:(r + 1) * LANES].astype(F32)
            shares = (values / column).astype(jnp.bfloat16).astype(F32)
            p_ref[s, r] = shares * l2_ref[r:r + 1, :]
        return carry


    big[...] = jnp.zeros_like(big)
    den[...] = jnp.zeros_like(den)
    pair_count = n_sample * (n_sample + 1) // 2
    inner = near * (near + 1) // 2

    def split(turn):
        across = turn - inner
        far = across - near * near
        within = jnp.where(far >= 0, far, turn)
        base = jnp.where(far >= 0, near, 0)
        j = lax.rem(within, near)
        i = lax.rem(j + within // near, near)
        is_across = (across >= 0) & (far < 0)
        i_block = jnp.where(is_across, across // near, base + i)
        j_block = jnp.where(is_across, near + lax.rem(across, near), base + j)
        return lax.bitwise_xor(my_s, i_block), lax.bitwise_xor(my_s, j_block)

    def place_sums(turn, sums):
        i_block, j_block = split(turn)
        now_big, now_den = big[j_block], den[j_block]
        for i in range(ROWS):
            here = lane == i_block * ROWS + i
            now_big = jnp.where(here, jnp.sum(sums[i], axis=1, keepdims=True), now_big)
            now_den = jnp.where(here, jnp.sum(sums[ROWS + i], axis=1, keepdims=True), now_den)
        big[j_block] = now_big
        den[j_block] = now_den

    def pairs(turn):
        i_block, j_block = split(turn)
        sums = [None] * (2 * ROWS)
        for r in range(depth):
            q = p_ref[j_block, r]
            for i in range(ROWS):
                p = p_ref[i_block, r, pl.ds(i, 1), :]
                summed = p + q
                inverse = lax.rsqrt(summed)
                top = jnp.maximum(p, q) * inverse
                low_part = summed * inverse
                if r == 0:
                    sums[i], sums[ROWS + i] = top, low_part
                else:
                    sums[i] += top
                    sums[ROWS + i] += low_part
        return tuple(sums)

    def advance(turn, sums):
        place_sums(turn - 1, sums)
        return pairs(turn)

    own_copy.wait()
    lax.fori_loop(0, near, arrive, 0)
    lax.fori_loop(0, near, prepare, 0, unroll=4)
    sums = lax.fori_loop(1, inner, advance, pairs(0), unroll=UNROLL)
    lax.fori_loop(near, n_sample, arrive, 0)
    lax.fori_loop(near, n_sample, prepare, 0, unroll=4)
    place_sums(pair_count - 1, lax.fori_loop(inner, pair_count, advance, sums, unroll=UNROLL))

    full = (n_sample * ROWS, LANES)
    row_block = lax.bitwise_xor(lax.broadcasted_iota(jnp.int32, full, 0) // ROWS, my_s)
    column_block = lax.bitwise_xor(lax.broadcasted_iota(jnp.int32, full, 1) // ROWS, my_s)
    row_at, column_at = row_block % near, column_block % near
    apart = (column_at - row_at + near) % near
    same = (row_block >= near) == (column_block >= near)
    turned = (2 * apart < near) | ((2 * apart == near) & (2 * row_at < near))
    mine = (same & turned) | ((row_block >= near) & (column_block < near))
    whole_big = big[...].reshape(full)
    whole_den = den[...].reshape(full)
    whole_big = jnp.where(mine, whole_big, whole_big.T)
    whole_den = jnp.where(mine, whole_den, whole_den.T)
    first = lax.broadcasted_iota(jnp.int32, full, 1) < half
    for t in range(n_branch):
        left = pltpu.roll(whole_big, (LANES - t * half) % LANES, 1) if t else whole_big
        shift = (LANES + half - t * half) % LANES
        right = pltpu.roll(whole_den, shift, 1) if shift else whole_den
        res_send[t] = jnp.where(first, left, right).reshape(n_sample, ROWS, LANES)

    def r_copy(flat, t, s, slot):
        return pltpu.make_async_remote_copy(
            src_ref=res_send.at[t, s],
            dst_ref=res_buf.at[slot],
            send_sem=r_send_sem.at[flat],
            recv_sem=r_recv_sem.at[slot],
            device_id=place(t, s),
            device_id_type=MESH,
        )

    def send_r(k, carry):
        flat, t, s = peer_at(k)
        r_copy(flat, t, s, me).start()
        return carry

    lax.fori_loop(1, n_dev, send_r, 0)
    res_buf[me] = res_send[my_t, my_s]

    def await_r(k, carry):
        flat, t, s = peer_at(k)
        r_copy(flat, t, s, flat).wait()
        return carry

    lax.fori_loop(1, n_dev, await_r, 0)
    total = res_buf[0]
    for k in range(1, n_dev):
        total = total + res_buf[k]
    out_ref[...] = total


def kernel_body(axes, n_branch, n_sample, abundance, length_table, branch_rows):
    width = abundance.shape[1]
    chunk = width // n_sample
    depth = chunk // LANES
    n_dev = n_branch * n_sample
    half = n_sample * ROWS // n_branch
    sums = pl.pallas_call(
        functools.partial(kernel, axes, n_branch, n_sample, chunk),
        out_shape=jax.ShapeDtypeStruct((ROWS, LANES), F32),
        in_specs=[pl.BlockSpec(memory_space=pl.ANY)] * 3,
        out_specs=pl.BlockSpec(memory_space=pltpu.VMEM),
        scratch_shapes=[
            pltpu.VMEM((ROWS, width), jnp.bfloat16),
            pltpu.VMEM((width // LANES, LANES), F32),
            pltpu.VMEM((depth, LANES), jnp.int32),
            pltpu.VMEM((n_sample, ROWS, chunk), jnp.bfloat16),
            pltpu.VMEM((1, LANES), F32),
            pltpu.VMEM((n_dev, 1, LANES), F32),
            pltpu.VMEM((n_sample, depth, ROWS, LANES), F32),
            pltpu.VMEM((depth, LANES), F32),
            pltpu.VMEM((n_sample, ROWS, LANES), F32),
            pltpu.VMEM((n_sample, ROWS, LANES), F32),
            pltpu.VMEM((n_branch, n_sample, ROWS, LANES), F32),
            pltpu.VMEM((n_dev, ROWS, LANES), F32),
            pltpu.SemaphoreType.DMA((3,)),
            pltpu.SemaphoreType.DMA,
            pltpu.SemaphoreType.DMA((n_sample,)),
            pltpu.SemaphoreType.DMA((n_sample,)),
            pltpu.SemaphoreType.DMA((n_dev,)),
            pltpu.SemaphoreType.DMA((n_dev,)),
            pltpu.SemaphoreType.DMA((n_dev,)),
            pltpu.SemaphoreType.DMA((n_dev,)),
        ],
        compiler_params=pltpu.CompilerParams(collective_id=0, has_side_effects=True),
    )(
        abundance,
        length_table.reshape(width // LANES, LANES),
        branch_rows.reshape(n_sample, depth, LANES),
    )
    big, den = sums[:, :half], sums[:, half:2 * half]
    return (2.0 * big - den) / den


def solution(mesh):
    n_branch, n_sample = mesh.shape["branch"], mesh.shape["sample"]
    axes = tuple(mesh.axis_names)

    def body(abundance, length_table, branch_rows):
        rows, width = abundance.shape
        fits = (
            rows == ROWS
            and n_sample * ROWS == LANES
            and n_branch > 1
            and LANES % n_branch == 0
            and width % (n_sample * ROWS * LANES) == 0
        )
        if not fits:
            return plain_body(abundance, length_table, branch_rows)
        return kernel_body(axes, n_branch, n_sample, abundance, length_table, branch_rows)

    placed = (P("sample", "branch"), P("branch"), P("branch"))
    return jax.shard_map(
        body, mesh=mesh, in_specs=placed, out_specs=P("sample", "branch"), check_vma=False
    )
```

```python
import functools

import jax
import jax.numpy as jnp
from jax import lax
from jax.experimental import pallas as pl
from jax.experimental.pallas import tpu as pltpu
from jax.sharding import PartitionSpec as P

MESH = pl.DeviceIdType.MESH
F32 = jnp.float32
ROWS = 8
LANES = 128
UNROLL = 16
STAGES = 4


def pair_sums(mine, other, lengths):
    count, width = mine.shape
    others = other.shape[0]
    block_size = width
    while block_size > 512 and block_size % 2 == 0 and (block_size * count * others > 2097152):
        block_size = block_size // 2
    block_count = width // block_size

    def absorb(carry, turn):
        begin = turn * block_size
        left = lax.dynamic_slice_in_dim(mine, begin, block_size, 1).astype(F32)[:, None, :]
        right = lax.dynamic_slice_in_dim(other, begin, block_size, 1).astype(F32)[None, :, :]
        weight = lax.dynamic_slice_in_dim(lengths, begin, block_size, 0)[None, None, :]
        summed = left + right
        inverse = lax.rsqrt(summed)
        return (
            (
                carry[0] + jnp.sum(weight * jnp.abs(left - right) * inverse, axis=2),
                carry[1] + jnp.sum(weight * summed * inverse, axis=2),
            ),
            None,
        )

    empty = jnp.zeros((count, others), F32)
    result, unused = lax.scan(absorb, (empty, empty), jnp.arange(block_count, dtype=jnp.int32))
    return result


def plain_body(abundance, length_table, branch_rows):
    values = abundance.astype(F32)
    totals = lax.psum(jnp.sum(values, axis=1), "branch")
    shares = (values / totals[:, None]).astype(jnp.bfloat16)
    lengths = jnp.take(length_table, branch_rows)
    numer_part, denom_part = pair_sums(
        shares, lax.all_gather(shares, "sample", axis=0, tiled=True), lengths
    )
    summed = (
        lax.psum_scatter(numer_part, "branch", scatter_dimension=1, tiled=True),
        lax.psum_scatter(denom_part, "branch", scatter_dimension=1, tiled=True),
    )
    return summed[0] / summed[1]


def kernel(
    axes, n_branch, n_sample, chunk,
    ab_hbm, table_hbm, rows_hbm, out_ref,
    ab, table, rows, x_buf, tot_send, tot_buf, p_ref, l2_ref, big, den, res_send, res_buf,
    local_sem, own_sem, x_send_sem, x_recv_sem, t_send_sem, t_recv_sem, r_send_sem, r_recv_sem,
):
    n_dev = n_branch * n_sample
    depth = chunk // LANES
    half = n_sample * ROWS // n_branch
    my_t = lax.axis_index("branch")
    my_s = lax.axis_index("sample")
    me = my_t * n_sample + my_s

    def place(t, s):
        where = {"branch": t, "sample": s}
        return tuple(where[name] for name in axes)

    def peer_at(k):
        flat = lax.bitwise_xor(me, k)
        return flat, flat // n_sample, lax.rem(flat, n_sample)

    ab_copy = pltpu.make_async_copy(ab_hbm, ab, local_sem.at[0])
    table_copy = pltpu.make_async_copy(table_hbm, table, local_sem.at[1])
    rows_copy = pltpu.make_async_copy(rows_hbm.at[my_s], rows, local_sem.at[2])
    own_copy = pltpu.make_async_copy(
        ab_hbm.at[:, pl.ds(pl.multiple_of(my_s * chunk, chunk), chunk)], x_buf.at[my_s], own_sem
    )
    ab_copy.start()
    table_copy.start()
    rows_copy.start()
    own_copy.start()

    barrier = pltpu.get_barrier_semaphore()

    def greet(k, carry):
        flat, t, s = peer_at(k)
        pl.semaphore_signal(barrier, inc=1, device_id=place(t, s), device_id_type=MESH)
        return carry

    lax.fori_loop(1, n_dev, greet, 0)

    def x_copy(to_s, slot, recv):
        return pltpu.make_async_remote_copy(
            src_ref=ab_hbm.at[:, pl.ds(pl.multiple_of(to_s * chunk, chunk), chunk)],
            dst_ref=x_buf.at[slot],
            send_sem=x_send_sem.at[to_s],
            recv_sem=x_recv_sem.at[recv],
            device_id=place(my_t, to_s),
            device_id_type=MESH,
        )

    def send_x(k, carry):
        x_copy(lax.bitwise_xor(my_s, k), my_s, my_s).start()
        return carry

    lane = lax.broadcasted_iota(jnp.int32, (ROWS, LANES), 1)
    sub = lax.broadcasted_iota(jnp.int32, (ROWS, LANES), 0)
    eye = lane == sub

    ab_copy.wait()
    step = min(chunk, 1024)

    def add_up(turn, acc):
        return acc + ab[:, pl.ds(pl.multiple_of(turn * step, step), step)].astype(F32)

    acc = lax.fori_loop(0, n_sample * chunk // step, add_up, jnp.zeros((ROWS, step), F32))
    part = jnp.sum(acc, axis=1, keepdims=True)
    line = jnp.sum(jnp.where(eye, part, 0.0), axis=0, keepdims=True)
    tot_send[...] = line
    tot_buf[me] = line

    def t_copy(flat, t, s, slot):
        return pltpu.make_async_remote_copy(
            src_ref=tot_send,
            dst_ref=tot_buf.at[slot],
            send_sem=t_send_sem.at[flat],
            recv_sem=t_recv_sem.at[slot],
            device_id=place(t, s),
            device_id_type=MESH,
        )

    def send_t(k, carry):
        flat, t, s = peer_at(k)
        t_copy(flat, t, s, me).start()
        return carry


    table_copy.wait()
    rows_copy.wait()
    index = rows[...]
    high, low = index // LANES, index % LANES

    def look_up(h, found):
        line = jnp.broadcast_to(table[pl.ds(h, 1), :], (depth, LANES))
        picked = jnp.take_along_axis(line, low, axis=1, mode="promise_in_bounds")
        return jnp.where(high == h, picked, found)

    lengths = lax.fori_loop(
        0, table.shape[0], look_up, jnp.zeros((depth, LANES), F32), unroll=8
    )
    l2_ref[...] = lengths * lengths

    pl.semaphore_wait(barrier, n_dev - 1)
    lax.fori_loop(1, n_dev, send_t, 0)
    lax.fori_loop(1, n_sample, send_x, 0)

    group = n_sample // STAGES

    def arrive(k, carry):
        s = lax.bitwise_xor(my_s, k)
        for t in range(n_branch):
            flat = t * n_sample + s

            @pl.when(flat != me)
            def _():
                t_copy(flat, t, s, flat).wait()

        @pl.when(k > 0)
        def _():
            x_copy(s, s, s).wait()

        return carry

    def prepare(k, carry):
        s = lax.bitwise_xor(my_s, k)
        total = tot_buf[s]
        for t in range(1, n_branch):
            total = total + tot_buf[t * n_sample + s]
        column = jnp.sum(
            jnp.where(eye, jnp.broadcast_to(total, (ROWS, LANES)), 0.0), axis=1, keepdims=True
        )
        for r in range(depth):
            values = x_buf[s, :, r * LANES:(r + 1) * LANES].astype(F32)
            shares = (values / column).astype(jnp.bfloat16).astype(F32)
            p_ref[s, r] = shares * l2_ref[r:r + 1, :]
        return carry


    big[...] = jnp.zeros_like(big)
    den[...] = jnp.zeros_like(den)
    within = group * (group + 1) // 2

    def split(stage, turn):
        base = stage * group
        across = turn - within
        j = lax.rem(turn, group)
        i = lax.rem(j + turn // group, group)
        i_block = jnp.where(across >= 0, across // group, base + i)
        j_block = base + jnp.where(across >= 0, lax.rem(across, group), j)
        return lax.bitwise_xor(my_s, i_block), lax.bitwise_xor(my_s, j_block)

    def place_sums(stage, turn, sums):
        i_block, j_block = split(stage, jnp.int32(turn))
        now_big, now_den = big[j_block], den[j_block]
        for i in range(ROWS):
            here = lane == i_block * ROWS + i
            now_big = jnp.where(here, jnp.sum(sums[i], axis=1, keepdims=True), now_big)
            now_den = jnp.where(here, jnp.sum(sums[ROWS + i], axis=1, keepdims=True), now_den)
        big[j_block] = now_big
        den[j_block] = now_den

    def pairs(stage, turn):
        i_block, j_block = split(stage, jnp.int32(turn))
        tops, lows = [], []
        others = [p_ref[j_block, r] for r in range(depth)]
        for i in range(ROWS):
            top = low_part = None
            for r in range(depth):
                p = p_ref[i_block, r, pl.ds(i, 1), :]
                q = others[r]
                summed = p + q
                inverse = lax.rsqrt(summed)
                more_top = jnp.maximum(p, q) * inverse
                more_low = summed * inverse
                top = more_top if r == 0 else top + more_top
                low_part = more_low if r == 0 else low_part + more_low
            tops.append(top)
            lows.append(low_part)
        return tuple(tops + lows)

    own_copy.wait()
    sums, before = None, None
    for stage in range(STAGES):
        count = within + stage * group * group
        head = count % UNROLL or UNROLL
        lax.fori_loop(stage * group, (stage + 1) * group, arrive, 0)
        lax.fori_loop(stage * group, (stage + 1) * group, prepare, 0, unroll=group)
        for turn in range(head):
            if before is not None:
                place_sums(*before, sums)
            sums, before = pairs(stage, turn), (stage, turn)

        def advance(loop, sums, stage=stage, head=head):
            for u in range(UNROLL):
                turn = head + loop * UNROLL + u
                place_sums(stage, turn - 1, sums)
                sums = pairs(stage, turn)
            return sums

        sums = lax.fori_loop(0, (count - head) // UNROLL, advance, sums)
        before = (stage, count - 1)
    place_sums(*before, sums)

    full = (n_sample * ROWS, LANES)
    row_block = lax.bitwise_xor(lax.broadcasted_iota(jnp.int32, full, 0) // ROWS, my_s)
    column_block = lax.bitwise_xor(lax.broadcasted_iota(jnp.int32, full, 1) // ROWS, my_s)
    row_at, column_at = row_block % group, column_block % group
    row_stage, column_stage = row_block // group, column_block // group
    apart = (column_at - row_at + group) % group
    turned = (2 * apart < group) | ((2 * apart == group) & (2 * row_at < group))
    mine = ((row_stage == column_stage) & turned) | (row_stage > column_stage)
    whole_big = big[...].reshape(full)
    whole_den = den[...].reshape(full)
    whole_big = jnp.where(mine, whole_big, whole_big.T)
    whole_den = jnp.where(mine, whole_den, whole_den.T)
    first = lax.broadcasted_iota(jnp.int32, full, 1) < half
    for t in range(n_branch):
        left = pltpu.roll(whole_big, (LANES - t * half) % LANES, 1) if t else whole_big
        shift = (LANES + half - t * half) % LANES
        right = pltpu.roll(whole_den, shift, 1) if shift else whole_den
        res_send[t] = jnp.where(first, left, right).reshape(n_sample, ROWS, LANES)

    def r_copy(flat, t, s, slot):
        return pltpu.make_async_remote_copy(
            src_ref=res_send.at[t, s],
            dst_ref=res_buf.at[slot],
            send_sem=r_send_sem.at[flat],
            recv_sem=r_recv_sem.at[slot],
            device_id=place(t, s),
            device_id_type=MESH,
        )

    def send_r(k, carry):
        flat, t, s = peer_at(k)
        r_copy(flat, t, s, me).start()
        return carry

    lax.fori_loop(1, n_dev, send_r, 0)
    res_buf[me] = res_send[my_t, my_s]

    def await_r(k, carry):
        flat, t, s = peer_at(k)
        r_copy(flat, t, s, flat).wait()
        return carry

    lax.fori_loop(1, n_dev, await_r, 0)
    total = res_buf[0]
    for k in range(1, n_dev):
        total = total + res_buf[k]
    out_ref[...] = total


def kernel_body(axes, n_branch, n_sample, abundance, length_table, branch_rows):
    width = abundance.shape[1]
    chunk = width // n_sample
    depth = chunk // LANES
    n_dev = n_branch * n_sample
    half = n_sample * ROWS // n_branch
    sums = pl.pallas_call(
        functools.partial(kernel, axes, n_branch, n_sample, chunk),
        out_shape=pltpu.VMEM((ROWS, LANES), F32),
        in_specs=[pl.BlockSpec(memory_space=pl.ANY)] * 3,
        out_specs=pl.BlockSpec(memory_space=pltpu.VMEM),
        scratch_shapes=[
            pltpu.VMEM((ROWS, width), jnp.bfloat16),
            pltpu.VMEM((width // LANES, LANES), F32),
            pltpu.VMEM((depth, LANES), jnp.int32),
            pltpu.VMEM((n_sample, ROWS, chunk), jnp.bfloat16),
            pltpu.VMEM((1, LANES), F32),
            pltpu.VMEM((n_dev, 1, LANES), F32),
            pltpu.VMEM((n_sample, depth, ROWS, LANES), F32),
            pltpu.VMEM((depth, LANES), F32),
            pltpu.VMEM((n_sample, ROWS, LANES), F32),
            pltpu.VMEM((n_sample, ROWS, LANES), F32),
            pltpu.VMEM((n_branch, n_sample, ROWS, LANES), F32),
            pltpu.VMEM((n_dev, ROWS, LANES), F32),
            pltpu.SemaphoreType.DMA((3,)),
            pltpu.SemaphoreType.DMA,
            pltpu.SemaphoreType.DMA((n_sample,)),
            pltpu.SemaphoreType.DMA((n_sample,)),
            pltpu.SemaphoreType.DMA((n_dev,)),
            pltpu.SemaphoreType.DMA((n_dev,)),
            pltpu.SemaphoreType.DMA((n_dev,)),
            pltpu.SemaphoreType.DMA((n_dev,)),
        ],
        compiler_params=pltpu.CompilerParams(collective_id=0, has_side_effects=True),
    )(
        abundance,
        length_table.reshape(width // LANES, LANES),
        branch_rows.reshape(n_sample, depth, LANES),
    )
    big, den = sums[:, :half], sums[:, half:2 * half]
    return (2.0 * big - den) / den


def solution(mesh):
    n_branch, n_sample = mesh.shape["branch"], mesh.shape["sample"]
    axes = tuple(mesh.axis_names)

    def body(abundance, length_table, branch_rows):
        rows, width = abundance.shape
        fits = (
            rows == ROWS
            and n_sample * ROWS == LANES
            and n_branch > 1
            and LANES % n_branch == 0
            and n_sample % STAGES == 0
            and width % (n_sample * ROWS * LANES) == 0
        )
        if not fits:
            return plain_body(abundance, length_table, branch_rows)
        return kernel_body(axes, n_branch, n_sample, abundance, length_table, branch_rows)

    placed = (P("sample", "branch"), P("branch"), P("branch"))
    return jax.shard_map(
        body, mesh=mesh, in_specs=placed, out_specs=P("sample", "branch"), check_vma=False
    )
```
